32 devices in a mesh: gz: 8 (over z, y), gy: 4 (over x, core).
Axes of the slice: x: 2, y: 2, z: 4, core: 2. Of those that a mesh axis runs over, the one named last changes fastest.
Arguments:
- charge: float32 [393216], P(('gz', 'gy')), may hold values from -4 to 4
- fractions: float32 [3, 393216], P(None, ('gz', 'gy')), may hold values from 0 to 1
- cell_base: int32 [3, 393216], P(None, ('gz', 'gy')), may hold values from 0 to 255, as said below
- live_blocks: int32 [8, 4], P('gz'), may hold values from 12 to 96, as said below
- send_blocks: int32 [8, 4], P('gz'), may hold values from 0 to 36, as said below
- moduli: float32 [3, 256], replicated, may hold values from 0.5 to 2
- screening: float32 [1], replicated, may hold values from 8 to 16
Outputs:
- forces: float32 [3, 393216], P(None, ('gz', 'gy'))
The draws below stay inside these ranges and needn't reach their ends.
Inputs may be any that keep to these rules, and one draw needn't show every extreme that they name: `cell_base`: row 0 lies in 0 to 31, row 1 in 0 to 63, row 2 in 0 to 255. `live_blocks`: a domain's live blocks are its first ones; in every row of the table some domain has 96 live blocks. send_blocks is at most the domain's live blocks; live_blocks minus send_blocks plus send_blocks of the domain before it along gy (cyclically) is at most 96; in every row some domain sends 36.
All inputs are finite; a program needn't handle non-finite values.
Results may differ from the reference program's by a relative error of at most 0.00023.
Values sent between devices are 32-bit elements; how exact they have to be, the bound alone decides.
No kernel may reach another device: no remote copies, remote signals or barrier semaphores. Data moves between devices by JAX's collectives and lax.ppermute only.
A program may use at most 128 MiB of HBM per device.

```python
import math
import jax
import jax.numpy as jnp

GRID = 256
BLOCK = 128
NBLK = 96
ATOMS_DEV = 12288
ATOMS = 393216
PZ = 32
PY = 64
SEND_MAX = 36
LOW = 12
N_GZ = 8
N_GY = 4


def migration_plan(key):
    base_key = jax.random.fold_in(key, 7)
    key_load, key_busy = jax.random.split(base_key)
    drawn = jax.random.randint(key_load, (N_GZ, N_GY), 0, 1001)
    powered = drawn * drawn // 1000
    powered = powered * powered // 1000
    live_count = LOW + (NBLK - LOW) * powered // 1000
    busiest = jax.random.randint(key_busy, (N_GZ, 1), 0, N_GY)
    lane_ids = jnp.arange(N_GY, dtype=jnp.int32)[None, :]
    live_count = jnp.where(lane_ids == busiest, NBLK, live_count)
    live_count = jnp.where(lane_ids == jnp.mod(busiest + 1, N_GY), LOW, live_count)
    following = jnp.roll(live_count, -1, axis=1)
    send_count = jnp.clip((live_count - following + 1) // 2, 0, SEND_MAX)
    return (live_count.astype(jnp.int32), send_count.astype(jnp.int32))


def draw_live_blocks(key, part):
    return migration_plan(key)[0]


def draw_send_blocks(key, part):
    return migration_plan(key)[1]


def draw_cell_base(key, part):
    key_z, key_y, key_x = jax.random.split(jax.random.fold_in(key, 11), 3)
    rows_z = jax.random.randint(key_z, (ATOMS,), 0, PZ)
    rows_y = jax.random.randint(key_y, (ATOMS,), 0, PY)
    rows_x = jax.random.randint(key_x, (ATOMS,), 0, GRID)
    return jnp.stack([rows_z, rows_y, rows_x]).astype(jnp.int32)


def steps_of(key, extent, cuts, low, high):
    def one(axis_at, shards_of):
        draws = jax.random.uniform(jax.random.fold_in(jax.random.fold_in(key, 6), axis_at), (shards_of,), jnp.float32, low / len(cuts), high / len(cuts))
        return jnp.repeat(jnp.exp(draws), extent[axis_at] // shards_of).reshape((-1,) + (1,) * (len(extent) - axis_at - 1))

    level = one(*cuts[0])
    for cut in cuts[1:]:
        level = level * one(*cut)
    return level


def normal_values(stream_key, shape, scale, limit, shards=(), held_as=jnp.bfloat16):
    factor_of = steps_of(stream_key, shape, shards, -0.22, 0.18) if shards else 1.0
    array = jax.random.normal(stream_key, shape, jnp.float32) * scale * factor_of
    return jnp.minimum(jnp.maximum(array, -limit), limit).astype(held_as)


def setup_inputs(seed: int = 0) -> dict:
    splits = jax.random.split(jax.random.key(seed), 8)
    charge = normal_values(splits[0], (ATOMS,), 1.0, 4.0, ((0, 32),), jnp.float32)
    fractions = jnp.clip(1.0 * jax.random.uniform(splits[1], (3, ATOMS), jnp.float32) ** steps_of(splits[1], (3, ATOMS), ((1, 32),), -0.2, 0.2), 0.0, 1.0)
    cell_base = draw_cell_base(jax.random.fold_in(splits[7], 71), 0)
    live_blocks = draw_live_blocks(jax.random.fold_in(splits[7], 71), 0)
    send_blocks = draw_send_blocks(jax.random.fold_in(splits[7], 71), 0)
    moduli = jnp.clip(jnp.exp(jax.random.uniform(splits[5], (3, GRID), jnp.float32, math.log(0.5), math.log(2.0))), 0.5, 2.0)
    screening = jnp.clip(jnp.exp(jax.random.uniform(splits[6], (1,), jnp.float32, math.log(8.0), math.log(16.0))), 8.0, 16.0)
    return {"charge": charge, "fractions": fractions, "cell_base": cell_base, "live_blocks": live_blocks, "send_blocks": send_blocks, "moduli": moduli, "screening": screening}


coulomb = 2.0


def spline_weights(fractions_row):
    remain = 1.0 - fractions_row
    square = fractions_row * fractions_row
    cubed = square * fractions_row
    weights = [remain * remain * remain / 6.0,
               (3.0 * cubed - 6.0 * square + 4.0) / 6.0,
               (-3.0 * cubed + 3.0 * square + 3.0 * fractions_row + 1.0) / 6.0,
               cubed / 6.0]
    slopes = [-0.5 * remain * remain,
              1.5 * square - 2.0 * fractions_row,
              -1.5 * square + fractions_row + 0.5,
              0.5 * square]
    return weights, slopes


def reference(charge, fractions, cell_base, live_blocks, send_blocks, moduli, screening):
    atom_index = jnp.arange(ATOMS, dtype=jnp.int32)
    device_index = atom_index // ATOMS_DEV
    slab_index = device_index // N_GY
    column_index = device_index % N_GY
    slot_index = atom_index % ATOMS_DEV
    live_count = live_blocks[slab_index, column_index]
    weighted = jnp.where(slot_index // BLOCK < live_count, charge, 0.0)
    weight_z, slope_z = spline_weights(fractions[0])
    weight_y, slope_y = spline_weights(fractions[1])
    weight_x, slope_x = spline_weights(fractions[2])
    base_z = slab_index * PZ + cell_base[0]
    base_y = column_index * PY + cell_base[1]
    base_x = cell_base[2]
    density = jnp.zeros((GRID * GRID * GRID,), jnp.float32)
    for shift_z in range(4):
        index_z = jnp.mod(base_z + shift_z, GRID)
        for shift_y in range(4):
            index_y = jnp.mod(base_y + shift_y, GRID)
            for shift_x in range(4):
                index_x = jnp.mod(base_x + shift_x, GRID)
                flat_index = ((index_z * GRID + index_y) * GRID + index_x).astype(jnp.int32)
                density = density.at[flat_index].add(weighted * weight_z[shift_z] * weight_y[shift_y] * weight_x[shift_x])
    density = density.reshape(GRID, GRID, GRID)
    spectrum = jnp.fft.fftn(density)
    waves = jnp.arange(GRID, dtype=jnp.int32)
    signed_wave = jnp.where(waves < GRID // 2, waves, waves - GRID)
    wave_square = signed_wave * signed_wave
    radius = wave_square[:, None, None] + wave_square[None, :, None] + wave_square[None, None, :]
    squared = radius.astype(jnp.float32) / float(GRID * GRID)
    product = coulomb * moduli[0][:, None, None] * moduli[1][None, :, None] * moduli[2][None, None, :]
    safe_squared = jnp.where(radius > 0, squared, 1.0)
    kernel = jnp.where(radius > 0, product * jnp.exp(-screening[0] * squared) / safe_squared, 0.0)
    potential = jnp.real(jnp.fft.ifftn(spectrum * kernel)).astype(jnp.float32)
    flat_potential = potential.reshape(-1)
    force_z = jnp.zeros((ATOMS,), jnp.float32)
    force_y = jnp.zeros((ATOMS,), jnp.float32)
    force_x = jnp.zeros((ATOMS,), jnp.float32)
    for shift_z in range(4):
        index_z = jnp.mod(base_z + shift_z, GRID)
        for shift_y in range(4):
            index_y = jnp.mod(base_y + shift_y, GRID)
            for shift_x in range(4):
                index_x = jnp.mod(base_x + shift_x, GRID)
                flat_index = ((index_z * GRID + index_y) * GRID + index_x).astype(jnp.int32)
                values = flat_potential[flat_index]
                force_z = force_z + slope_z[shift_z] * weight_y[shift_y] * weight_x[shift_x] * values
                force_y = force_y + weight_z[shift_z] * slope_y[shift_y] * weight_x[shift_x] * values
                force_x = force_x + weight_z[shift_z] * weight_y[shift_y] * slope_x[shift_x] * values
    home = -weighted[None, :] * jnp.stack([force_z, force_y, force_x])
    domains = N_GZ * N_GY
    home = home.reshape(3, domains, ATOMS_DEV)
    live_flat = live_blocks.reshape(-1)
    send_flat = send_blocks.reshape(-1)
    devices = jnp.arange(domains, dtype=jnp.int32)
    column_of = devices % N_GY
    previous = (devices - column_of + jnp.mod(column_of - 1, N_GY)).astype(jnp.int32)
    kept_atoms = (live_flat - send_flat) * BLOCK
    arriving = send_flat[previous] * BLOCK
    source_start = (live_flat[previous] - send_flat[previous]) * BLOCK
    slots = jnp.arange(ATOMS_DEV, dtype=jnp.int32)
    own_forces = jnp.where(slots[None, None, :] < kept_atoms[None, :, None], home, 0.0)
    guest_slot = slots[None, :] - kept_atoms[:, None] + source_start[:, None]
    valid = (slots[None, :] >= kept_atoms[:, None]) & (slots[None, :] < kept_atoms[:, None] + arriving[:, None])
    guest_slot = jnp.clip(guest_slot, 0, ATOMS_DEV - 1).astype(jnp.int32)
    neighbour = home[:, previous, :]
    guest = jnp.take_along_axis(neighbour, guest_slot[None, :, :], axis=2)
    result = own_forces + jnp.where(valid[None, :, :], guest, 0.0)
    return result.reshape(3, ATOMS)
```

```python
import functools

import jax
import jax.numpy as jnp
import numpy as np
from jax import lax
from jax.experimental import pallas as pl
from jax.experimental.pallas import tpu as pltpu
from jax.sharding import PartitionSpec as P

GRID = 256
BLOCK = 128
SEND_MAX = 36
CHUNK = 512
PLANES = 6

high = lax.Precision.HIGH
coulomb = 2.0


def shifted(x, axis, by):
    peers = lax.axis_size(axis)
    return lax.ppermute(x, axis, [(i, (i + by) % peers) for i in range(peers)])


def spline_weights(fractions_row):
    remain = 1.0 - fractions_row
    square = fractions_row * fractions_row
    cubed = square * fractions_row
    return [
        remain * remain * remain * (1.0 / 6.0),
        (3.0 * cubed - 6.0 * square + 4.0) * (1.0 / 6.0),
        (-3.0 * cubed + 3.0 * square + 3.0 * fractions_row + 1.0) * (1.0 / 6.0),
        cubed * (1.0 / 6.0),
    ]


def spline_slopes(fractions_row):
    remain = 1.0 - fractions_row
    square = fractions_row * fractions_row
    return [
        -0.5 * remain * remain,
        1.5 * square - 2.0 * fractions_row,
        -1.5 * square + fractions_row + 0.5,
        0.5 * square,
    ]


def stencil_table(cell_row, weights, span_cells, wrap_around):
    offset = lax.broadcasted_iota(jnp.int32, (span_cells, cell_row.shape[1]), 0) - cell_row
    if wrap_around:
        offset = jnp.where(offset < 0, offset + span_cells, offset)
    stencil = jnp.where(offset == 0, weights[0], 0.0)
    for shift_k in range(1, 4):
        stencil = jnp.where(offset == shift_k, weights[shift_k], stencil)
    return stencil


def halves(x):
    upper = x.astype(jnp.bfloat16)
    lower = (x - upper.astype(jnp.float32)).astype(jnp.bfloat16)
    return upper, lower


def product3(left, right, dims):
    def one(a, b):
        return lax.dot_general(a, b, (dims, ((), ())), preferred_element_type=jnp.float32)

    return one(left[0], right[0]) + (one(left[0], right[1]) + one(left[1], right[0]))


def masked_charge(live_ref, charge_ref, chunk):
    slots = pl.program_id(0) * chunk + lax.broadcasted_iota(jnp.int32, (1, chunk), 1)
    return jnp.where(slots < live_ref[0] * BLOCK, charge_ref[...], 0.0)


def spread_kernel(live_ref, charge_ref, fractions_ref, cells_ref, tile_ref, z_ref, *, row_count):
    chunk = charge_ref.shape[1]
    z_count = z_ref.shape[0]
    group_rows = PLANES * row_count

    @pl.when(pl.program_id(0) == 0)
    def _():
        tile_ref[...] = jnp.zeros_like(tile_ref)

    @pl.when(pl.program_id(0) * chunk < live_ref[0] * BLOCK)
    def _():
        charge = masked_charge(live_ref, charge_ref, chunk)
        weight_z = [w * charge for w in spline_weights(fractions_ref[0:1, :])]
        z_ref[...] = stencil_table(cells_ref[0:1, :], weight_z, z_count, False)
        table_y = stencil_table(
            cells_ref[1:2, :], spline_weights(fractions_ref[1:2, :]), row_count, False
        )
        table_x = halves(
            stencil_table(cells_ref[2:3, :], spline_weights(fractions_ref[2:3, :]), GRID, True)
        )

        @pl.loop(0, z_count // PLANES)
        def _(group):
            plane = jnp.concatenate(
                [z_ref[pl.ds(group * PLANES + p, 1), :] * table_y for p in range(PLANES)], 0
            )
            rows = pl.ds(pl.multiple_of(group * group_rows, 8), group_rows)
            tile_ref[rows, :] += product3(halves(plane), table_x, ((1,), (1,)))


def gather_kernel(
    live_ref,
    charge_ref,
    fractions_ref,
    cells_ref,
    padded_ref,
    forces_ref,
    upper_ref,
    lower_ref,
    z_ref,
    rise_ref,
    *,
    row_count,
):
    chunk = charge_ref.shape[1]
    z_count = z_ref.shape[0]
    group_rows = PLANES * row_count

    @pl.when(pl.program_id(0) == 0)
    def _():
        @pl.loop(0, z_count // PLANES)
        def _(group):
            rows = pl.ds(pl.multiple_of(group * group_rows, 16), group_rows)
            upper, lower = halves(padded_ref[rows, :])
            upper_ref[rows, :] = upper
            lower_ref[rows, :] = lower

    is_live = pl.program_id(0) * chunk < live_ref[0] * BLOCK

    @pl.when(jnp.logical_not(is_live))
    def _():
        forces_ref[...] = jnp.zeros_like(forces_ref)

    @pl.when(is_live)
    def _():
        charge = masked_charge(live_ref, charge_ref, chunk)
        z_row, y_row, x_row = (fractions_ref[c : c + 1, :] for c in range(3))
        z_cell, y_cell, x_cell = (cells_ref[c : c + 1, :] for c in range(3))
        z_ref[...] = stencil_table(z_cell, spline_weights(z_row), z_count, False)
        rise_ref[...] = stencil_table(z_cell, spline_slopes(z_row), z_count, False)
        table_y = stencil_table(y_cell, spline_weights(y_row), row_count, False)
        rise_y = stencil_table(y_cell, spline_slopes(y_row), row_count, False)
        table_x = halves(stencil_table(x_cell, spline_weights(x_row), GRID, True))
        rise_x = halves(stencil_table(x_cell, spline_slopes(x_row), GRID, True))

        def folded(table, field, p):
            part = table * field[p * row_count : (p + 1) * row_count]
            total = part[0:8]
            for start in range(8, row_count, 8):
                total = total + part[start : start + 8]
            return total

        def step(group, sums):
            rows = pl.ds(pl.multiple_of(group * group_rows, 16), group_rows)
            field = (upper_ref[rows, :], lower_ref[rows, :])
            along_weight = product3(field, table_x, ((1,), (0,)))
            along_slope = product3(field, rise_x, ((1,), (0,)))
            sum_z, sum_y, sum_x = sums
            for p in range(PLANES):
                plane_z = z_ref[pl.ds(group * PLANES + p, 1), :]
                plane_rise = rise_ref[pl.ds(group * PLANES + p, 1), :]
                sum_z = sum_z + plane_rise * folded(table_y, along_weight, p)
                sum_y = sum_y + plane_z * folded(rise_y, along_weight, p)
                sum_x = sum_x + plane_z * folded(table_y, along_slope, p)
            return sum_z, sum_y, sum_x

        empty = jnp.zeros((8, chunk), jnp.float32)
        sums = lax.fori_loop(0, z_count // PLANES, step, (empty, empty, empty))
        forces_ref[...] = jnp.concatenate(
            [-charge * jnp.sum(s, axis=0, keepdims=True) for s in sums], 0
        )


def atom_specs(chunk):
    return [
        pl.BlockSpec(memory_space=pltpu.SMEM),
        pl.BlockSpec((1, chunk), lambda i: (0, i)),
        pl.BlockSpec((3, chunk), lambda i: (0, i)),
        pl.BlockSpec((3, chunk), lambda i: (0, i)),
    ]


def spread(live, charge, fractions, cells, z_count, row_count):
    atoms = charge.shape[1]
    rows = z_count * row_count
    return pl.pallas_call(
        functools.partial(spread_kernel, row_count=row_count),
        grid=(atoms // CHUNK,),
        in_specs=atom_specs(CHUNK),
        out_specs=pl.BlockSpec((rows, GRID), lambda i: (0, 0)),
        out_shape=jax.ShapeDtypeStruct((rows, GRID), jnp.float32),
        scratch_shapes=[pltpu.VMEM((z_count, CHUNK), jnp.float32)],
        name="spread",
    )(live, charge, fractions, cells)


def gather(live, charge, fractions, cells, padded, z_count, row_count):
    atoms = charge.shape[1]
    rows = z_count * row_count
    return pl.pallas_call(
        functools.partial(gather_kernel, row_count=row_count),
        grid=(atoms // CHUNK,),
        in_specs=atom_specs(CHUNK) + [pl.BlockSpec((rows, GRID), lambda i: (0, 0))],
        out_specs=pl.BlockSpec((3, CHUNK), lambda i: (0, i)),
        out_shape=jax.ShapeDtypeStruct((3, atoms), jnp.float32),
        scratch_shapes=[
            pltpu.VMEM((rows, GRID), jnp.bfloat16),
            pltpu.VMEM((rows, GRID), jnp.bfloat16),
            pltpu.VMEM((z_count, CHUNK), jnp.float32),
            pltpu.VMEM((z_count, CHUNK), jnp.float32),
        ],
        name="gather",
    )(live, charge, fractions, cells, padded)


def dft_tables():
    counter = np.arange(GRID)
    angles = 2.0 * np.pi / GRID * ((counter[:, None] * counter[None, :]) % GRID)
    return jnp.asarray(np.cos(angles), jnp.float32), jnp.asarray(np.sin(angles), jnp.float32)


def complex_table(cosine, sine, inverse, split_in, split_out):
    sign = 1.0 if inverse else -1.0
    if inverse:
        cosine = cosine * (1.0 / GRID)
        sine = sine * (1.0 / GRID)
    table = jnp.stack(
        [jnp.stack([cosine, sign * sine]), jnp.stack([-sign * sine, cosine])]
    )
    table = table.reshape(2, 2, split_in, GRID // split_in, split_out, GRID // split_out)
    return table.transpose(2, 0, 3, 4, 1, 5).reshape(2 * GRID, 2 * GRID)


def signed_wave(waves):
    return jnp.where(waves < GRID // 2, waves, waves - GRID)


def influence(moduli, screening, first_x, first_z, count_kx, count_kz):
    index_x = first_x + lax.iota(jnp.int32, count_kx)
    index_z = first_z + lax.iota(jnp.int32, count_kz)
    wave_x = signed_wave(index_x)
    wave_z = signed_wave(index_z)
    wave_y = signed_wave(lax.iota(jnp.int32, GRID))
    radius = (
        (wave_x * wave_x)[:, None, None]
        + (wave_z * wave_z)[None, :, None]
        + (wave_y * wave_y)[None, None, :]
    )
    squared = radius.astype(jnp.float32) / float(GRID * GRID)
    mirrored = jnp.roll(moduli[:, ::-1], 1, axis=1)

    def outer(table):
        modulus_x = lax.dynamic_slice_in_dim(
            jnp.pad(table[2], (0, count_kx)), first_x, count_kx, 0
        )
        modulus_z = lax.dynamic_slice_in_dim(table[0], first_z, count_kz, 0)
        return modulus_z[None, :, None] * table[1][None, None, :] * modulus_x[:, None, None]

    product = (0.5 * coulomb) * (outer(moduli) + outer(mirrored))
    safe_squared = jnp.where(radius > 0, squared, 1.0)
    return jnp.where(radius > 0, product * jnp.exp(-screening[0] * squared) / safe_squared, 0.0)


def matmul(left, right, dims):
    return lax.dot_general(
        left, right, (dims, ((), ())), precision=high, preferred_element_type=jnp.float32
    )


def potential_field(grid_block, moduli, screening, slab_index, column_index):
    slabs = lax.axis_size("gz")
    columns = lax.axis_size("gy")
    planes, rows, _ = grid_block.shape
    half = GRID // 2 + 1
    kxl = -(-half // slabs)
    kzl = GRID // columns
    cosine, sine = dft_tables()

    index_x = lax.iota(jnp.int32, kxl * slabs)
    pad = kxl * slabs - half
    weight = jnp.where(
        index_x < half, jnp.where((index_x == 0) | (index_x == half - 1), 1.0, 2.0), 0.0
    )
    cos_half = jnp.pad(cosine[:half], ((0, pad), (0, 0)))
    sin_half = jnp.pad(sine[:half], ((0, pad), (0, 0)))
    stacked = jnp.stack([cos_half, -sin_half]).reshape(2, slabs, kxl, GRID)
    real_table = stacked.transpose(1, 0, 2, 3).reshape(slabs * 2 * kxl, GRID)
    scaled = stacked * (weight / GRID).reshape(1, slabs, kxl, 1)
    real_back = scaled.transpose(1, 0, 2, 3).reshape(slabs * 2 * kxl, GRID)

    z_table = complex_table(cosine, sine, False, slabs, columns)
    y_table = complex_table(cosine, sine, False, columns, 1)
    y_back = complex_table(cosine, sine, True, 1, columns)
    z_back = complex_table(cosine, sine, True, columns, slabs)

    field = matmul(grid_block.reshape(planes * rows, GRID), real_table, ((1,), (1,)))
    field = field.reshape(planes, rows, slabs, 2, kxl).transpose(2, 3, 0, 4, 1)
    field = field.reshape(slabs, 2 * planes, kxl * rows)
    field = lax.all_to_all(field, "gz", split_axis=0, concat_axis=0, tiled=True)
    field = field.reshape(2 * GRID, kxl * rows)
    field = matmul(z_table, field, ((0,), (0,)))
    field = field.reshape(columns, 2 * kzl, kxl * rows)
    field = lax.all_to_all(field, "gy", split_axis=0, concat_axis=0, tiled=True)
    field = field.reshape(columns, 2, kzl, kxl, rows).transpose(3, 2, 0, 1, 4)
    field = field.reshape(kxl * kzl, 2 * GRID)
    field = matmul(field, y_table, ((1,), (0,)))
    kernel = influence(moduli, screening, slab_index * kxl, column_index * kzl, kxl, kzl)
    kernel = kernel.reshape(kxl * kzl, GRID)
    field = field * jnp.concatenate([kernel, kernel], 1)
    field = matmul(y_back, field, ((0,), (1,)))
    field = field.reshape(columns, 2 * rows, kxl * kzl)
    field = lax.all_to_all(field, "gy", split_axis=0, concat_axis=0, tiled=True)
    field = field.reshape(columns, 2, rows, kxl, kzl).transpose(3, 2, 0, 1, 4)
    field = field.reshape(kxl * rows, 2 * GRID)
    field = matmul(z_back, field, ((0,), (1,)))
    field = field.reshape(slabs, 2 * planes, kxl * rows)
    field = lax.all_to_all(field, "gz", split_axis=0, concat_axis=0, tiled=True)
    field = field.reshape(slabs, 2, planes, kxl, rows).transpose(2, 4, 0, 1, 3)
    field = field.reshape(planes * rows, slabs * 2 * kxl)
    return matmul(field, real_back, ((1,), (0,))).reshape(planes, rows, GRID)


def body(charge, fractions, cell_base, live_blocks, send_blocks, moduli, screening):
    slab_count = lax.axis_size("gz")
    column_count = lax.axis_size("gy")
    planes = GRID // slab_count
    rows = GRID // column_count
    row_count = -(-(rows + 3) // 8) * 8
    z_count = -(-(planes + 3) // PLANES) * PLANES
    slab_index = lax.axis_index("gz")
    column_index = lax.axis_index("gy")
    lane_ids = lax.iota(jnp.int32, column_count)
    live_count = jnp.sum(jnp.where(lane_ids == column_index, live_blocks[0], 0))
    send_count = jnp.sum(jnp.where(lane_ids == column_index, send_blocks[0], 0))
    before = jnp.sum(
        jnp.where(lane_ids == jnp.mod(column_index - 1, column_count), send_blocks[0], 0)
    )
    kept_atoms = (live_count - send_count) * BLOCK
    live = live_count.reshape(1)
    charge_row = charge[None, :]

    volume = spread(live, charge_row, fractions, cell_base, z_count, row_count)
    volume = volume.reshape(z_count, row_count, GRID)
    rim_planes = shifted(volume[planes : planes + 3], "gz", 1)
    volume = jnp.concatenate([volume[:3] + rim_planes, volume[3:planes]], 0)
    rim_rows = shifted(volume[:, rows : rows + 3], "gy", 1)
    grid_block = jnp.concatenate([volume[:, :3] + rim_rows, volume[:, 3:rows]], 1)

    potential = potential_field(grid_block, moduli, screening, slab_index, column_index)

    upper_rows = shifted(potential[:, :3], "gy", -1)
    spare = jnp.zeros((planes, row_count - rows - 3, GRID), jnp.float32)
    widened = jnp.concatenate([potential, upper_rows, spare], 1)
    upper_planes = shifted(widened[:3], "gz", -1)
    spare = jnp.zeros((z_count - planes - 3, row_count, GRID), jnp.float32)
    padded = jnp.concatenate([widened, upper_planes, spare], 0)
    padded = padded.reshape(z_count * row_count, GRID)

    home = gather(live, charge_row, fractions, cell_base, padded, z_count, row_count)
    margin = SEND_MAX * BLOCK
    atoms = home.shape[1]
    lent = lax.dynamic_slice_in_dim(jnp.pad(home, ((0, 0), (0, margin))), kept_atoms, margin, 1)
    arrivals = shifted(lent, "gy", 1)
    slots = lax.iota(jnp.int32, margin)
    arrivals = jnp.where(slots[None, :] < before * BLOCK, arrivals, 0.0)
    own = jnp.where(lax.iota(jnp.int32, atoms)[None, :] < kept_atoms, home, 0.0)
    holder = jnp.zeros((3, atoms + margin), jnp.float32)
    zero = jnp.zeros((), jnp.int32)
    holder = lax.dynamic_update_slice(holder, arrivals, (zero, kept_atoms))
    return own + holder[:, :atoms]


def solution(mesh):
    return jax.shard_map(
        body,
        mesh=mesh,
        in_specs=(
            P(("gz", "gy")),
            P(None, ("gz", "gy")),
            P(None, ("gz", "gy")),
            P("gz", None),
            P("gz", None),
            P(),
            P(),
        ),
        out_specs=P(None, ("gz", "gy")),
        check_vma=False,
    )
```

```python
import functools

import jax
import jax.numpy as jnp
import numpy as np
from jax import lax
from jax.experimental import pallas as pl
from jax.experimental.pallas import tpu as pltpu
from jax.sharding import PartitionSpec as P

GRID = 256
BLOCK = 128
SEND_MAX = 36
CHUNK = 512
PLANES = 4

high = lax.Precision.HIGH
coulomb = 2.0


def shifted(x, axis, by):
    peers = lax.axis_size(axis)
    return lax.ppermute(x, axis, [(i, (i + by) % peers) for i in range(peers)])


def spline_weights(fractions_row):
    remain = 1.0 - fractions_row
    square = fractions_row * fractions_row
    cubed = square * fractions_row
    return [
        remain * remain * remain * (1.0 / 6.0),
        (3.0 * cubed - 6.0 * square + 4.0) * (1.0 / 6.0),
        (-3.0 * cubed + 3.0 * square + 3.0 * fractions_row + 1.0) * (1.0 / 6.0),
        cubed * (1.0 / 6.0),
    ]


def spline_slopes(fractions_row):
    remain = 1.0 - fractions_row
    square = fractions_row * fractions_row
    return [
        -0.5 * remain * remain,
        1.5 * square - 2.0 * fractions_row,
        -1.5 * square + fractions_row + 0.5,
        0.5 * square,
    ]


def stencil_table(cell_row, weights, span_cells, wrap_around):
    offset = lax.broadcasted_iota(jnp.int32, (span_cells, cell_row.shape[1]), 0) - cell_row
    if wrap_around:
        offset = jnp.where(offset < 0, offset + span_cells, offset)
    stencil = jnp.where(offset == 0, weights[0], 0.0)
    for shift_k in range(1, 4):
        stencil = jnp.where(offset == shift_k, weights[shift_k], stencil)
    return stencil


def halves(x):
    upper = x.astype(jnp.bfloat16)
    lower = (x - upper.astype(jnp.float32)).astype(jnp.bfloat16)
    return upper, lower


def product3(left, right, dims):
    def one(a, b):
        return lax.dot_general(a, b, (dims, ((), ())), preferred_element_type=jnp.float32)

    return one(left[0], right[0]) + (one(left[0], right[1]) + one(left[1], right[0]))


def masked_charge(live_ref, charge_ref, chunk):
    slots = pl.program_id(0) * chunk + lax.broadcasted_iota(jnp.int32, (1, chunk), 1)
    return jnp.where(slots < live_ref[0] * BLOCK, charge_ref[...], 0.0)


def group_range(live_ref):
    chunk_at = pl.program_id(0)
    return live_ref[1 + chunk_at], live_ref[1 + pl.num_programs(0) + chunk_at]


def plane_bounds(live_count, cell_z):
    chunks = cell_z.reshape(-1, CHUNK)
    first = jnp.min(chunks, axis=1) // PLANES
    last = jnp.max(jnp.where(chunks < GRID, chunks, 0), axis=1)
    return jnp.concatenate([live_count.reshape(1), first, (last + 3) // PLANES + 1])


def spread_kernel(live_ref, charge_ref, fractions_ref, cells_ref, tile_ref, z_ref, *, row_count):
    chunk = charge_ref.shape[1]
    z_count = z_ref.shape[0]
    group_rows = PLANES * row_count

    @pl.when(pl.program_id(0) == 0)
    def _():
        tile_ref[...] = jnp.zeros_like(tile_ref)

    @pl.when(pl.program_id(0) * chunk < live_ref[0] * BLOCK)
    def _():
        charge = masked_charge(live_ref, charge_ref, chunk)
        weight_z = [w * charge for w in spline_weights(fractions_ref[0:1, :])]
        z_ref[...] = stencil_table(cells_ref[0:1, :], weight_z, z_count, False)
        table_y = stencil_table(
            cells_ref[1:2, :], spline_weights(fractions_ref[1:2, :]), row_count, False
        )
        table_x = halves(
            stencil_table(cells_ref[2:3, :], spline_weights(fractions_ref[2:3, :]), GRID, True)
        )

        @pl.loop(*group_range(live_ref))
        def _(group):
            plane = jnp.concatenate(
                [z_ref[pl.ds(group * PLANES + p, 1), :] * table_y for p in range(PLANES)], 0
            )
            rows = pl.ds(pl.multiple_of(group * group_rows, 8), group_rows)
            tile_ref[rows, :] += product3(halves(plane), table_x, ((1,), (1,)))


def gather_kernel(
    live_ref,
    charge_ref,
    fractions_ref,
    cells_ref,
    padded_ref,
    forces_ref,
    upper_ref,
    lower_ref,
    z_ref,
    rise_ref,
    *,
    row_count,
):
    chunk = charge_ref.shape[1]
    z_count = z_ref.shape[0]
    group_rows = PLANES * row_count

    @pl.when(pl.program_id(0) == 0)
    def _():
        @pl.loop(0, z_count // PLANES)
        def _(group):
            rows = pl.ds(pl.multiple_of(group * group_rows, 16), group_rows)
            upper, lower = halves(padded_ref[rows, :])
            upper_ref[rows, :] = upper
            lower_ref[rows, :] = lower

    is_live = pl.program_id(0) * chunk < live_ref[0] * BLOCK

    @pl.when(jnp.logical_not(is_live))
    def _():
        forces_ref[...] = jnp.zeros_like(forces_ref)

    @pl.when(is_live)
    def _():
        charge = masked_charge(live_ref, charge_ref, chunk)
        z_row, y_row, x_row = (fractions_ref[c : c + 1, :] for c in range(3))
        z_cell, y_cell, x_cell = (cells_ref[c : c + 1, :] for c in range(3))
        z_ref[...] = stencil_table(z_cell, spline_weights(z_row), z_count, False)
        rise_ref[...] = stencil_table(z_cell, spline_slopes(z_row), z_count, False)
        table_y = stencil_table(y_cell, spline_weights(y_row), row_count, False)
        rise_y = stencil_table(y_cell, spline_slopes(y_row), row_count, False)
        table_x = halves(stencil_table(x_cell, spline_weights(x_row), GRID, True))
        rise_x = halves(stencil_table(x_cell, spline_slopes(x_row), GRID, True))

        def folded(table, field, p):
            part = table * field[p * row_count : (p + 1) * row_count]
            total = part[0:8]
            for start in range(8, row_count, 8):
                total = total + part[start : start + 8]
            return total

        def step(group, sums):
            rows = pl.ds(pl.multiple_of(group * group_rows, 16), group_rows)
            field = (upper_ref[rows, :], lower_ref[rows, :])
            along_weight = product3(field, table_x, ((1,), (0,)))
            along_slope = product3(field, rise_x, ((1,), (0,)))
            sum_z, sum_y, sum_x = sums
            for p in range(PLANES):
                plane_z = z_ref[pl.ds(group * PLANES + p, 1), :]
                plane_rise = rise_ref[pl.ds(group * PLANES + p, 1), :]
                sum_z = sum_z + plane_rise * folded(table_y, along_weight, p)
                sum_y = sum_y + plane_z * folded(rise_y, along_weight, p)
                sum_x = sum_x + plane_z * folded(table_y, along_slope, p)
            return sum_z, sum_y, sum_x

        empty = jnp.zeros((8, chunk), jnp.float32)
        sums = lax.fori_loop(*group_range(live_ref), step, (empty, empty, empty))
        forces_ref[...] = jnp.concatenate(
            [-charge * jnp.sum(s, axis=0, keepdims=True) for s in sums], 0
        )


def atom_specs(chunk):
    return [
        pl.BlockSpec(memory_space=pltpu.SMEM),
        pl.BlockSpec((1, chunk), lambda i: (0, i)),
        pl.BlockSpec((3, chunk), lambda i: (0, i)),
        pl.BlockSpec((3, chunk), lambda i: (0, i)),
    ]


def spread(live, charge, fractions, cells, z_count, row_count):
    atoms = charge.shape[1]
    rows = z_count * row_count
    return pl.pallas_call(
        functools.partial(spread_kernel, row_count=row_count),
        grid=(atoms // CHUNK,),
        in_specs=atom_specs(CHUNK),
        out_specs=pl.BlockSpec((rows, GRID), lambda i: (0, 0)),
        out_shape=jax.ShapeDtypeStruct((rows, GRID), jnp.float32),
        scratch_shapes=[pltpu.VMEM((z_count, CHUNK), jnp.float32)],
        name="spread",
    )(live, charge, fractions, cells)


def gather(live, charge, fractions, cells, padded, z_count, row_count):
    atoms = charge.shape[1]
    rows = z_count * row_count
    return pl.pallas_call(
        functools.partial(gather_kernel, row_count=row_count),
        grid=(atoms // CHUNK,),
        in_specs=atom_specs(CHUNK) + [pl.BlockSpec((rows, GRID), lambda i: (0, 0))],
        out_specs=pl.BlockSpec((3, CHUNK), lambda i: (0, i)),
        out_shape=jax.ShapeDtypeStruct((3, atoms), jnp.float32),
        scratch_shapes=[
            pltpu.VMEM((rows, GRID), jnp.bfloat16),
            pltpu.VMEM((rows, GRID), jnp.bfloat16),
            pltpu.VMEM((z_count, CHUNK), jnp.float32),
            pltpu.VMEM((z_count, CHUNK), jnp.float32),
        ],
        name="gather",
    )(live, charge, fractions, cells, padded)


def dft_tables():
    counter = np.arange(GRID)
    angles = 2.0 * np.pi / GRID * ((counter[:, None] * counter[None, :]) % GRID)
    return jnp.asarray(np.cos(angles), jnp.float32), jnp.asarray(np.sin(angles), jnp.float32)


def complex_table(cosine, sine, inverse, split_in, split_out):
    sign = 1.0 if inverse else -1.0
    if inverse:
        cosine = cosine * (1.0 / GRID)
        sine = sine * (1.0 / GRID)
    table = jnp.stack(
        [jnp.stack([cosine, sign * sine]), jnp.stack([-sign * sine, cosine])]
    )
    table = table.reshape(2, 2, split_in, GRID // split_in, split_out, GRID // split_out)
    return table.transpose(2, 0, 3, 4, 1, 5).reshape(2 * GRID, 2 * GRID)


def signed_wave(waves):
    return jnp.where(waves < GRID // 2, waves, waves - GRID)


def influence(moduli, screening, first_x, first_z, count_kx, count_kz):
    index_x = first_x + lax.iota(jnp.int32, count_kx)
    index_z = first_z + lax.iota(jnp.int32, count_kz)
    wave_x = signed_wave(index_x)
    wave_z = signed_wave(index_z)
    wave_y = signed_wave(lax.iota(jnp.int32, GRID))
    radius = (
        (wave_x * wave_x)[:, None, None]
        + (wave_z * wave_z)[None, :, None]
        + (wave_y * wave_y)[None, None, :]
    )
    squared = radius.astype(jnp.float32) / float(GRID * GRID)
    mirrored = jnp.roll(moduli[:, ::-1], 1, axis=1)

    def outer(table):
        modulus_x = lax.dynamic_slice_in_dim(
            jnp.pad(table[2], (0, count_kx)), first_x, count_kx, 0
        )
        modulus_z = lax.dynamic_slice_in_dim(table[0], first_z, count_kz, 0)
        return modulus_z[None, :, None] * table[1][None, None, :] * modulus_x[:, None, None]

    product = (0.5 * coulomb) * (outer(moduli) + outer(mirrored))
    safe_squared = jnp.where(radius > 0, squared, 1.0)
    return jnp.where(radius > 0, product * jnp.exp(-screening[0] * squared) / safe_squared, 0.0)


def matmul(left, right, dims):
    return lax.dot_general(
        left, right, (dims, ((), ())), precision=high, preferred_element_type=jnp.float32
    )


def potential_field(grid_block, moduli, screening, slab_index, column_index):
    slabs = lax.axis_size("gz")
    columns = lax.axis_size("gy")
    planes, rows, _ = grid_block.shape
    half = GRID // 2 + 1
    kxl = -(-half // slabs)
    kzl = GRID // columns
    cosine, sine = dft_tables()

    index_x = lax.iota(jnp.int32, kxl * slabs)
    pad = kxl * slabs - half
    weight = jnp.where(
        index_x < half, jnp.where((index_x == 0) | (index_x == half - 1), 1.0, 2.0), 0.0
    )
    cos_half = jnp.pad(cosine[:half], ((0, pad), (0, 0)))
    sin_half = jnp.pad(sine[:half], ((0, pad), (0, 0)))
    stacked = jnp.stack([cos_half, -sin_half]).reshape(2, slabs, kxl, GRID)
    real_table = stacked.transpose(1, 0, 2, 3).reshape(slabs * 2 * kxl, GRID)
    scaled = stacked * (weight / GRID).reshape(1, slabs, kxl, 1)
    real_back = scaled.transpose(1, 0, 2, 3).reshape(slabs * 2 * kxl, GRID)

    z_table = complex_table(cosine, sine, False, slabs, columns)
    y_table = complex_table(cosine, sine, False, columns, 1)
    y_back = complex_table(cosine, sine, True, 1, columns)
    z_back = complex_table(cosine, sine, True, columns, slabs)

    field = matmul(grid_block.reshape(planes * rows, GRID), real_table, ((1,), (1,)))
    field = field.reshape(planes, rows, slabs, 2, kxl).transpose(2, 3, 0, 4, 1)
    field = field.reshape(slabs, 2 * planes, kxl * rows)
    field = lax.all_to_all(field, "gz", split_axis=0, concat_axis=0, tiled=True)
    field = field.reshape(2 * GRID, kxl * rows)
    field = matmul(z_table, field, ((0,), (0,)))
    field = field.reshape(columns, 2 * kzl, kxl * rows)
    field = lax.all_to_all(field, "gy", split_axis=0, concat_axis=0, tiled=True)
    field = field.reshape(columns, 2, kzl, kxl, rows).transpose(3, 2, 0, 1, 4)
    field = field.reshape(kxl * kzl, 2 * GRID)
    field = matmul(field, y_table, ((1,), (0,)))
    kernel = influence(moduli, screening, slab_index * kxl, column_index * kzl, kxl, kzl)
    kernel = kernel.reshape(kxl * kzl, GRID)
    field = field * jnp.concatenate([kernel, kernel], 1)
    field = matmul(y_back, field, ((0,), (1,)))
    field = field.reshape(columns, 2 * rows, kxl * kzl)
    field = lax.all_to_all(field, "gy", split_axis=0, concat_axis=0, tiled=True)
    field = field.reshape(columns, 2, rows, kxl, kzl).transpose(3, 2, 0, 1, 4)
    field = field.reshape(kxl * rows, 2 * GRID)
    field = matmul(z_back, field, ((0,), (1,)))
    field = field.reshape(slabs, 2 * planes, kxl * rows)
    field = lax.all_to_all(field, "gz", split_axis=0, concat_axis=0, tiled=True)
    field = field.reshape(slabs, 2, planes, kxl, rows).transpose(2, 4, 0, 1, 3)
    field = field.reshape(planes * rows, slabs * 2 * kxl)
    return matmul(field, real_back, ((1,), (0,))).reshape(planes, rows, GRID)


def body(charge, fractions, cell_base, live_blocks, send_blocks, moduli, screening):
    slab_count = lax.axis_size("gz")
    column_count = lax.axis_size("gy")
    planes = GRID // slab_count
    rows = GRID // column_count
    row_count = -(-(rows + 3) // 8) * 8
    z_count = -(-(planes + 3) // PLANES) * PLANES
    slab_index = lax.axis_index("gz")
    column_index = lax.axis_index("gy")
    lane_ids = lax.iota(jnp.int32, column_count)
    live_count = jnp.sum(jnp.where(lane_ids == column_index, live_blocks[0], 0))
    send_count = jnp.sum(jnp.where(lane_ids == column_index, send_blocks[0], 0))
    before = jnp.sum(
        jnp.where(lane_ids == jnp.mod(column_index - 1, column_count), send_blocks[0], 0)
    )
    kept_atoms = (live_count - send_count) * BLOCK
    slots = lax.iota(jnp.int32, charge.shape[0])
    cell_z = jnp.where(slots < live_count * BLOCK, cell_base[0], GRID)
    ordered = lax.sort(
        (cell_z, slots, charge, *fractions, cell_base[1], cell_base[2]),
        num_keys=1,
        is_stable=False,
    )
    origin = ordered[1]
    charge_row = ordered[2][None, :]
    fractions = jnp.stack(ordered[3:6])
    cell_base = jnp.stack([ordered[0], ordered[6], ordered[7]])
    live = plane_bounds(live_count, ordered[0])

    volume = spread(live, charge_row, fractions, cell_base, z_count, row_count)
    volume = volume.reshape(z_count, row_count, GRID)
    rim_planes = shifted(volume[planes : planes + 3], "gz", 1)
    volume = jnp.concatenate([volume[:3] + rim_planes, volume[3:planes]], 0)
    rim_rows = shifted(volume[:, rows : rows + 3], "gy", 1)
    grid_block = jnp.concatenate([volume[:, :3] + rim_rows, volume[:, 3:rows]], 1)

    potential = potential_field(grid_block, moduli, screening, slab_index, column_index)

    upper_rows = shifted(potential[:, :3], "gy", -1)
    spare = jnp.zeros((planes, row_count - rows - 3, GRID), jnp.float32)
    widened = jnp.concatenate([potential, upper_rows, spare], 1)
    upper_planes = shifted(widened[:3], "gz", -1)
    spare = jnp.zeros((z_count - planes - 3, row_count, GRID), jnp.float32)
    padded = jnp.concatenate([widened, upper_planes, spare], 0)
    padded = padded.reshape(z_count * row_count, GRID)

    home = gather(live, charge_row, fractions, cell_base, padded, z_count, row_count)
    home = jnp.stack(lax.sort((origin, *home), num_keys=1, is_stable=False)[1:])
    margin = SEND_MAX * BLOCK
    atoms = home.shape[1]
    lent = lax.dynamic_slice_in_dim(jnp.pad(home, ((0, 0), (0, margin))), kept_atoms, margin, 1)
    arrivals = shifted(lent, "gy", 1)
    slots = lax.iota(jnp.int32, margin)
    arrivals = jnp.where(slots[None, :] < before * BLOCK, arrivals, 0.0)
    own = jnp.where(lax.iota(jnp.int32, atoms)[None, :] < kept_atoms, home, 0.0)
    holder = jnp.zeros((3, atoms + margin), jnp.float32)
    zero = jnp.zeros((), jnp.int32)
    holder = lax.dynamic_update_slice(holder, arrivals, (zero, kept_atoms))
    return own + holder[:, :atoms]


def solution(mesh):
    return jax.shard_map(
        body,
        mesh=mesh,
        in_specs=(
            P(("gz", "gy")),
            P(None, ("gz", "gy")),
            P(None, ("gz", "gy")),
            P("gz", None),
            P("gz", None),
            P(),
            P(),
        ),
        out_specs=P(None, ("gz", "gy")),
        check_vma=False,
    )
```
